32 devices in a mesh: grp: 2 (over x), wk: 16 (over z, y, core).
Axes of the slice: x: 2, y: 2, z: 4, core: 2. Of those that a mesh axis runs over, the one named last changes fastest.
Arguments:
- grads: bfloat16 [2, 4, 512, 1024], P('grp', None, 'wk'), may hold values from -4 to 4
- bank: bfloat16 [16, 5, 512, 512], P('wk'), as said below
- owners: int32 [4], replicated, may hold values from 0 to 15, as said below
- col_map: int32 [4, 2], replicated, may hold values from 0 to 3
Outputs:
- update: float32 [4, 512, 1024], P(None, 'grp', 'wk')
The draws below stay inside these ranges and needn't reach their ends.
Inputs may be any that keep to these rules, and one draw needn't show every extreme that they name: `owners`: 4 distinct worker indices; the last worker serves one of the layers. `bank`: every block is symmetric.
All inputs are finite; a program needn't handle non-finite values.
Results may differ from the reference program's by a relative error of at most 0.015.
Values may be sent and summed in bfloat16 or wider, within the bound.
No kernel may reach another device: no remote copies, remote signals or barrier semaphores. Data moves between devices by JAX's collectives and lax.ppermute only.
A program may use at most 64 MiB of HBM per device.

```python
import math
import jax
import jax.numpy as jnp
from jax import lax

B = 512
COLB = 2
OUTB = 4
LAYERS = 4
WIDTH = 1024
N_GRP = 2
N_WK = 16


def draw_bank(key, part):
    first_key = jax.random.fold_in(key, 11)
    second_key = jax.random.fold_in(key, 23)
    shape = (N_WK, OUTB + 1, B, B)
    raw = jax.random.normal(first_key, shape, jnp.float32) * 0.6
    diagonal = jnp.exp(jax.random.uniform(second_key, (N_WK, OUTB + 1, B), jnp.float32, math.log(0.5), math.log(2.0)))
    symmetric = (raw + jnp.swapaxes(raw, -1, -2)) * (0.7071 / math.sqrt(B))
    identity = jnp.eye(B, dtype=jnp.float32)
    return (symmetric * (1.0 - identity) + identity * diagonal[..., None]).astype(jnp.bfloat16)


def draw_owners(key, part):
    first_key = jax.random.fold_in(key, 31)
    second_key = jax.random.fold_in(key, 47)
    others = jax.random.permutation(first_key, N_WK - 1)[:LAYERS - 1].astype(jnp.int32)
    values = jnp.concatenate([others, jnp.full((1,), N_WK - 1, jnp.int32)])
    order = jax.random.permutation(second_key, LAYERS).astype(jnp.int32)
    return values[order].astype(jnp.int32)


def with_ends(drawn, key, low, top_value):
    shape = drawn.shape
    place = [jax.random.randint(jax.random.fold_in(key, axis), (), 0, shape[axis]) for axis in range(len(shape))]
    drawn = drawn.at[tuple(place)].set(low)
    longest = shape.index(max(shape))
    place[longest] = (place[longest] + 1) % shape[longest]
    return drawn.at[tuple(place)].set(top_value)


def shard_levels(own_key, extent, split, smallest, top_value):
    factor_of, own = 1.0, jax.random.fold_in(own_key, 6)
    for axis_at, shards_of in split:
        heights = jnp.exp(jax.random.uniform(jax.random.fold_in(own, axis_at), (shards_of,), jnp.float32, smallest / len(split), top_value / len(split)))
        factor_of = factor_of * jnp.repeat(heights, extent[axis_at] // shards_of).reshape([-1 if axis == axis_at else 1 for axis in range(len(extent))])
    return factor_of


def noise(key, shape, width, most, shards=(), kind=jnp.bfloat16):
    gain = shard_levels(key, shape, shards, -0.22, 0.18) if shards else 1.0
    entries = jax.random.normal(key, shape, jnp.float32) * width * gain
    return jnp.minimum(jnp.maximum(entries, -most), most).astype(kind)


def setup_inputs(seed: int = 0) -> dict:
    keys = jax.random.split(jax.random.key(seed), 5)
    return {
        "grads": noise(keys[0], (N_GRP, LAYERS, B, WIDTH), 0.5, 4.0, ((0, 2), (2, 16))),
        "bank": draw_bank(jax.random.fold_in(keys[4], 71), 0),
        "owners": draw_owners(jax.random.fold_in(keys[4], 71), 0),
        "col_map": with_ends(jax.random.randint(keys[3], (LAYERS, COLB), 0, OUTB), jax.random.fold_in(keys[3], 1), 0, OUTB - 1).astype(jnp.int32),
    }


def right_multiply(rows_in, right_blocks):
    rows_count = rows_in.shape[0]
    split_rows = rows_in.astype(jnp.float32).reshape(rows_count, COLB, B)
    mixed = jnp.einsum("nkb,kbc->nkc", split_rows, right_blocks.astype(jnp.float32))
    return mixed.reshape(rows_count, COLB * B).astype(jnp.bfloat16)


def reference(grads, bank, owners, col_map):
    results = []
    for layer_index in range(LAYERS):
        factors = bank[owners[layer_index]]
        left_inverse = factors[0]
        right_blocks = jnp.take(factors[1:], col_map[layer_index], axis=0)
        summed = jnp.sum(grads[:, layer_index].astype(jnp.float32), axis=0).astype(jnp.bfloat16)
        summed = lax.optimization_barrier(summed)
        mixed = right_multiply(summed, right_blocks)
        results.append(jnp.dot(left_inverse, mixed, preferred_element_type=jnp.float32))
    return jnp.stack(results)
```

```python
import jax
import jax.numpy as jnp
from jax import lax
from jax.sharding import PartitionSpec as P


def shifted(value, axis, shift):
    size = lax.axis_size(axis)
    return lax.ppermute(value, axis, [(i, (i + shift) % size) for i in range(size)])


def summed_columns(rows, axis):
    groups = lax.axis_size(axis)
    me = lax.axis_index(axis)
    width = rows.shape[-1] // groups

    def columns(index):
        return lax.dynamic_slice_in_dim(rows, index * width, width, rows.ndim - 1)

    total = columns(me).astype(jnp.float32)
    for shift in range(1, groups):
        total += shifted(columns((me + shift) % groups), axis, shift).astype(jnp.float32)
    return total.astype(jnp.bfloat16)


def swap_rows_for_columns(columns_by_rows, axis):
    groups = lax.axis_size(axis)
    me = lax.axis_index(axis)
    columns, rows = columns_by_rows.shape
    share = rows // groups

    def piece(index):
        return lax.dynamic_slice_in_dim(columns_by_rows, index * share, share, 1)

    full = jnp.zeros((groups * columns, share), columns_by_rows.dtype)
    for shift in range(groups):
        sent = piece((me + shift) % groups)
        got = shifted(sent, axis, shift) if shift else sent
        full = lax.dynamic_update_slice_in_dim(full, got, ((me - shift) % groups) * columns, 0)
    return full


def on_device(grads, bank, owners, col_map):
    layers = grads.shape[1]
    block = bank.shape[2]
    workers = lax.axis_size("wk")
    worker = lax.axis_index("wk")

    summed = summed_columns(grads[0], "grp")

    serves = owners[None, :] == jnp.arange(workers, dtype=owners.dtype)[:, None]
    outgoing = jnp.zeros((workers,) + summed.shape[1:], summed.dtype)
    for layer in range(layers):
        outgoing = jnp.where(serves[:, layer, None, None], summed[layer][None], outgoing)
    gathered = lax.all_to_all(outgoing, "wk", 0, 0, tiled=True).reshape(block, -1)

    my_layer = jnp.sum(jnp.where(owners == worker, jnp.arange(layers), 0))
    left = bank[0, 0]
    left_product = lax.dot_general(
        gathered, left, (((0,), (0,)), ((), ())), preferred_element_type=jnp.float32
    ).astype(jnp.bfloat16)
    left_product = swap_rows_for_columns(left_product, "grp")
    pieces = []
    for index in range(col_map.shape[1]):
        right = lax.dynamic_index_in_dim(bank[0], 1 + col_map[my_layer, index], 0, False)
        part = left_product[index * block : (index + 1) * block]
        pieces.append(jnp.dot(right, part, preferred_element_type=jnp.float32).astype(jnp.bfloat16))
    product = jnp.concatenate(pieces, axis=0)

    product = product.reshape(workers, -1, product.shape[1])
    returned = lax.all_to_all(product, "wk", 0, 0, tiled=True)
    results = []
    for layer in range(layers):
        part = lax.dynamic_index_in_dim(returned, owners[layer], 0, False)
        results.append(part.astype(jnp.float32).T)
    return jnp.stack(results)


def solution(mesh):
    in_specs = (P("grp", None, "wk", None), P("wk", None, None, None), P(), P())
    out_specs = P(None, "grp", "wk")
    return jax.shard_map(
        on_device, mesh=mesh, in_specs=in_specs, out_specs=out_specs, check_vma=False
    )
```

```python
import jax
import jax.numpy as jnp
from jax import lax
from jax.sharding import PartitionSpec as P


def shifted(value, axis, shift):
    size = lax.axis_size(axis)
    return lax.ppermute(value, axis, [(i, (i + shift) % size) for i in range(size)])


def on_device(grads, bank, owners, col_map):
    layers, _, total_width = grads.shape[1:]
    block = bank.shape[2]
    groups, workers = lax.axis_size("grp"), lax.axis_size("wk")
    me, worker = lax.axis_index("grp"), lax.axis_index("wk")
    width = total_width // groups
    share = block // groups

    def columns(group):
        return lax.dynamic_slice_in_dim(grads[0], group * width, width, 2)

    summed = columns(me).astype(jnp.float32)
    for shift in range(1, groups):
        summed += shifted(columns((me + shift) % groups), "grp", shift).astype(jnp.float32)
    summed = summed.astype(jnp.bfloat16)

    serves = owners[None, :] == jnp.arange(workers, dtype=owners.dtype)[:, None]
    outgoing = jnp.broadcast_to(summed[0], (workers,) + summed.shape[1:])
    for layer in range(1, layers):
        outgoing = jnp.where(serves[:, layer, None, None], summed[layer][None], outgoing)
    gathered = lax.all_to_all(outgoing, "wk", 0, 0, tiled=True).reshape(block, width)

    my_layer = jnp.sum(jnp.where(owners == worker, jnp.arange(layers), 0))
    left = bank[0, 0]
    products = [None] * groups
    for shift in reversed(range(groups)):
        rows = lax.dynamic_slice_in_dim(left, (me + shift) % groups * share, share, 0)
        product = jnp.dot(rows, gathered, preferred_element_type=jnp.float32)
        product = product.astype(jnp.bfloat16)
        products[shift] = shifted(product, "grp", shift) if shift else product
    blocks = col_map.shape[1]
    full = jnp.zeros((groups, share, width), jnp.bfloat16)
    for shift in range(groups):
        full = lax.dynamic_update_slice_in_dim(
            full, products[shift][None], (me + groups - shift) % groups, 0
        )
    full = full.transpose(1, 0, 2).reshape(share, blocks, block)
    rights = jnp.stack(
        [
            lax.dynamic_index_in_dim(bank[0], 1 + col_map[my_layer, index], 0, False)
            for index in range(blocks)
        ]
    )
    product = jnp.einsum("jab,rjb->jar", rights, full, preferred_element_type=jnp.float32)
    product = product.astype(jnp.bfloat16)

    product = product.reshape(workers, -1, share)
    returned = lax.all_to_all(product, "wk", 0, 0, tiled=True)
    results = []
    for layer in range(layers):
        part = lax.dynamic_index_in_dim(returned, owners[layer], 0, False)
        results.append(part.astype(jnp.float32).T)
    return jnp.stack(results)


def solution(mesh):
    in_specs = (P("grp", None, "wk", None), P("wk", None, None, None), P(), P())
    out_specs = P(None, "grp", "wk")
    return jax.shard_map(
        on_device, mesh=mesh, in_specs=in_specs, out_specs=out_specs, check_vma=False
    )
```

```python
import jax
import jax.numpy as jnp
from jax import lax
from jax.sharding import PartitionSpec as P


def shifted(value, axis, shift):
    size = lax.axis_size(axis)
    return lax.ppermute(value, axis, [(i, (i + shift) % size) for i in range(size)])


def pick(stack, index):
    return lax.dynamic_index_in_dim(stack, index, 0, False)


def returned_by_parts(gathered, bank, owners, my_columns):
    block = bank.shape[2]
    groups, workers = lax.axis_size("grp"), lax.axis_size("wk")
    me, worker = lax.axis_index("grp"), lax.axis_index("wk")
    size = workers // groups
    part, places = worker // size, owners % size

    share = block // groups
    left, right = lax.optimization_barrier((bank[0, 0], pick(bank[0], 1 + my_columns[me])))
    left_product = jnp.dot(left, gathered, preferred_element_type=jnp.float32)
    left_product = left_product.astype(jnp.bfloat16).reshape(groups, share, block)
    rights = jnp.broadcast_to(right, (groups,) + right.shape)
    product = jnp.einsum("gab,grb->gar", rights, left_product, preferred_element_type=jnp.float32)
    product = product.astype(jnp.bfloat16).reshape(workers, -1, share)

    parts = [
        [group * workers + index * size + place for group in range(groups) for place in range(size)]
        for index in range(groups)
    ]
    arrived = lax.all_to_all(
        product, ("grp", "wk"), 0, 0, axis_index_groups=parts, tiled=True
    ).reshape(groups, size, -1, share)

    def layers_of(index):
        return jnp.stack([pick(pick(arrived, index), place) for place in places])

    result = layers_of(part)
    for shift in range(1, groups):
        other = shifted(layers_of((part + shift) % groups), "wk", shift * size)
        theirs = owners // size == (part + groups - shift) % groups
        result = jnp.where(theirs[:, None, None], other, result)
    return result


def returned_by_rows(gathered, bank, owners, my_columns):
    block = bank.shape[2]
    width = gathered.shape[1]
    groups, workers = lax.axis_size("grp"), lax.axis_size("wk")
    me = lax.axis_index("grp")
    share, blocks = block // groups, my_columns.shape[0]

    full = jnp.zeros((groups, share, width), jnp.bfloat16)
    for shift in reversed(range(groups)):
        rows = lax.dynamic_slice_in_dim(bank[0, 0], (me + shift) % groups * share, share, 0)
        product = jnp.dot(rows, gathered, preferred_element_type=jnp.float32)
        product = product.astype(jnp.bfloat16)
        product = shifted(product, "grp", shift) if shift else product
        source = (me + groups - shift) % groups
        full = lax.dynamic_update_slice_in_dim(full, product[None], source, 0)
    full = full.transpose(1, 0, 2).reshape(share, blocks, block)
    rights = jnp.stack([pick(bank[0], 1 + my_columns[index]) for index in range(blocks)])
    product = jnp.einsum("jab,rjb->jar", rights, full, preferred_element_type=jnp.float32)
    product = product.astype(jnp.bfloat16).reshape(workers, -1, share)
    arrived = lax.all_to_all(product, "wk", 0, 0, tiled=True)
    return jnp.stack([pick(arrived, owner) for owner in owners])


def on_device(grads, bank, owners, col_map):
    layers, _, total_width = grads.shape[1:]
    block = bank.shape[2]
    groups, workers = lax.axis_size("grp"), lax.axis_size("wk")
    me, worker = lax.axis_index("grp"), lax.axis_index("wk")
    width = total_width // groups

    serves = owners[None, :] == jnp.arange(workers, dtype=owners.dtype)[:, None]

    def columns(group):
        return lax.dynamic_slice_in_dim(grads[0], group * width, width, 2)

    def placed(rows):
        placed_rows = jnp.broadcast_to(rows[0], (workers,) + rows.shape[1:])
        for layer in range(1, layers):
            placed_rows = jnp.where(serves[:, layer, None, None], rows[layer][None], placed_rows)
        return placed_rows.astype(jnp.float32)

    summed = placed(columns(me))
    for shift in range(1, groups):
        summed += placed(shifted(columns((me + shift) % groups), "grp", shift))
    outgoing = summed.astype(jnp.bfloat16)
    gathered = lax.all_to_all(outgoing, "wk", 0, 0, tiled=True).reshape(block, width)

    my_layer = jnp.sum(jnp.where(owners == worker, jnp.arange(layers), 0))
    by_parts = width == block and workers % groups == 0
    returned = returned_by_parts if by_parts else returned_by_rows
    result = returned(gathered, bank, owners, pick(col_map, my_layer))
    return result.astype(jnp.float32).transpose(0, 2, 1)


def solution(mesh):
    in_specs = (P("grp", None, "wk", None), P("wk", None, None, None), P(), P())
    out_specs = P(None, "grp", "wk")
    return jax.shard_map(
        on_device, mesh=mesh, in_specs=in_specs, out_specs=out_specs, check_vma=False
    )
```

```python
import jax
import jax.numpy as jnp
import numpy as np
from jax import lax
from jax.sharding import PartitionSpec as P

MEMBER_ORDERS = {
    8: (3, 6, 1, 5, 2, 0, 7, 4),
    16: (11, 6, 13, 9, 10, 5, 8, 0, 15, 2, 12, 4, 3, 14, 1, 7),
}


def member_order(size):
    return np.array(MEMBER_ORDERS.get(size, range(size)), np.int32)


def shifted(value, axis, shift):
    size = lax.axis_size(axis)
    return lax.ppermute(value, axis, [(i, (i + shift) % size) for i in range(size)])


def pick(stack, index):
    return lax.dynamic_index_in_dim(stack, index, 0, False)


def scalars_of(values, limit):
    count = values.shape[0]
    if limit**count > 2**31:
        return [values[index] for index in range(count)]
    packed = jnp.sum(values * np.array([limit**index for index in range(count)], np.int32))
    return [packed // limit**index % limit for index in range(count)]


def looked_up(index, table):
    value = jnp.asarray(table[0], jnp.int32)
    for at in range(1, len(table)):
        value = jnp.where(index == at, table[at], value)
    return value


def in_order(rows, order):
    pieces = rows.reshape(len(order), -1, rows.shape[-1])
    return jnp.take(pieces, order, axis=0).reshape(rows.shape)


def transposed_dot(left, right):
    return lax.dot_general(
        left, right, (((0,), (0,)), ((), ())), preferred_element_type=jnp.float32
    ).astype(jnp.bfloat16)


def returned_by_parts(gathered, left, bank, owners, my_columns):
    block = bank.shape[2]
    groups, workers = lax.axis_size("grp"), lax.axis_size("wk")
    me, worker = lax.axis_index("grp"), lax.axis_index("wk")
    size = workers // groups
    share = block // groups
    order = member_order(size)
    part = worker // size
    places = [looked_up(owner % size, np.argsort(order).tolist()) for owner in owners]

    right = in_order(pick(bank[0], 1 + jnp.sum(jnp.where(jnp.arange(groups) == me, my_columns, 0))), order)
    left, right = lax.optimization_barrier((left, right))
    left_product = transposed_dot(gathered, left)
    product = [
        jnp.dot(
            right,
            left_product[:, group * share : (group + 1) * share],
            preferred_element_type=jnp.float32,
        ).astype(jnp.bfloat16)
        for group in range(groups)
    ]
    product = jnp.stack(product).reshape(workers, -1, share)

    parts = [
        [group * workers + index * size + int(place) for group in range(groups) for place in order]
        for index in range(groups)
    ]
    arrived = lax.all_to_all(
        product, ("grp", "wk"), 0, 0, axis_index_groups=parts, tiled=True
    ).reshape(groups, size, -1, share)

    def layers_of(index):
        return jnp.stack([pick(pick(arrived, index), place) for place in places])

    result = layers_of(part)
    for shift in range(1, groups):
        other = shifted(layers_of((part + shift) % groups), "wk", shift * size)
        source = (part + groups - shift) % groups
        theirs = jnp.stack([owner // size == source for owner in owners])
        result = jnp.where(theirs[:, None, None], other, result)
    return result


def returned_by_rows(gathered, left, bank, owners, my_columns):
    block = bank.shape[2]
    width = gathered.shape[1]
    groups, workers = lax.axis_size("grp"), lax.axis_size("wk")
    me = lax.axis_index("grp")
    share, blocks = block // groups, my_columns.shape[0]

    full = jnp.zeros((groups, share, width), jnp.bfloat16)
    for shift in reversed(range(groups)):
        rows = lax.dynamic_slice_in_dim(left, (me + shift) % groups * share, share, 1)
        product = transposed_dot(rows, gathered)
        product = shifted(product, "grp", shift) if shift else product
        source = (me + groups - shift) % groups
        full = lax.dynamic_update_slice_in_dim(full, product[None], source, 0)
    full = full.transpose(1, 0, 2).reshape(share, blocks, block)
    rights = jnp.stack([pick(bank[0], 1 + my_columns[index]) for index in range(blocks)])
    product = jnp.einsum("jab,rjb->jar", rights, full, preferred_element_type=jnp.float32)
    product = product.astype(jnp.bfloat16).reshape(workers, -1, share)
    arrived = lax.all_to_all(product, "wk", 0, 0, tiled=True)
    return jnp.stack([pick(arrived, owner) for owner in owners])


def on_device(grads, bank, owners, col_map):
    layers, _, total_width = grads.shape[1:]
    block = bank.shape[2]
    groups, workers = lax.axis_size("grp"), lax.axis_size("wk")
    me, worker = lax.axis_index("grp"), lax.axis_index("wk")
    width = total_width // groups
    order = member_order(workers)

    serves = owners[None, :] == order[:, None]

    def columns(group):
        return lax.dynamic_slice_in_dim(grads[0], group * width, width, 2)

    def placed(rows):
        placed_rows = jnp.broadcast_to(rows[0], (workers,) + rows.shape[1:])
        for layer in range(1, layers):
            placed_rows = jnp.where(serves[:, layer, None, None], rows[layer][None], placed_rows)
        return placed_rows.astype(jnp.float32)

    summed = placed(columns(me))
    for shift in range(1, groups):
        summed += placed(shifted(columns((me + shift) % groups), "grp", shift))
    outgoing = summed.astype(jnp.bfloat16)
    planes = [[group * workers + int(member) for member in order] for group in range(groups)]
    gathered = lax.all_to_all(
        outgoing, ("grp", "wk"), 0, 0, axis_index_groups=planes, tiled=True
    ).reshape(block, width)

    my_columns = jnp.sum(jnp.where((owners == worker)[:, None], col_map, 0), axis=0)
    owners = scalars_of(owners, workers)
    left = in_order(bank[0, 0], order)
    by_parts = width == block and workers % groups == 0
    returned = returned_by_parts if by_parts else returned_by_rows
    result = returned(gathered, left, bank, owners, my_columns)
    return result.astype(jnp.float32).transpose(0, 2, 1)


def solution(mesh):
    in_specs = (P("grp", None, "wk", None), P("wk", None, None, None), P(), P())
    out_specs = P(None, "grp", "wk")
    return jax.shard_map(
        on_device, mesh=mesh, in_specs=in_specs, out_specs=out_specs, check_vma=False
    )
```

```python
import jax
import jax.numpy as jnp
import numpy as np
from jax import lax
from jax.experimental import pallas as pl
from jax.experimental.pallas import tpu as pltpu
from jax.sharding import PartitionSpec as P

MEMBER_ORDERS = {
    8: (7, 0, 1, 5, 2, 6, 3, 4),
    16: (11, 7, 13, 2, 6, 10, 5, 8, 12, 15, 9, 4, 3, 14, 1, 0),
}


def member_order(size):
    return np.array(MEMBER_ORDERS.get(size, range(size)), np.int32)


def shifted(value, axis, shift):
    size = lax.axis_size(axis)
    return lax.ppermute(value, axis, [(i, (i + shift) % size) for i in range(size)])


def pick(stack, index):
    return lax.dynamic_index_in_dim(stack, index, 0, False)


def scalars_of(values, limit):
    count = values.shape[0]
    if limit**count > 2**31:
        return [values[index] for index in range(count)]
    packed = jnp.sum(values * np.array([limit**index for index in range(count)], np.int32))
    return [packed // limit**index % limit for index in range(count)]


def looked_up(index, table):
    value = jnp.asarray(table[0], jnp.int32)
    for at in range(1, len(table)):
        value = jnp.where(index == at, table[at], value)
    return value


def in_order(rows, order):
    pieces = rows.reshape(len(order), -1, rows.shape[-1])
    return jnp.take(pieces, order, axis=0).reshape(rows.shape)


def transposed_dot(left, right):
    return lax.dot_general(
        left, right, (((0,), (0,)), ((), ())), preferred_element_type=jnp.float32
    ).astype(jnp.bfloat16)


def products_kernel(gathered_ref, left_ref, right_ref, product_ref):
    mixed = lax.dot_general(
        right_ref[...],
        gathered_ref[...],
        (((1,), (1,)), ((), ())),
        preferred_element_type=jnp.float32,
    ).astype(jnp.bfloat16)
    groups, _, share = product_ref.shape
    for group in range(groups):
        product_ref[group] = jnp.dot(
            mixed,
            left_ref[:, group * share : (group + 1) * share],
            preferred_element_type=jnp.float32,
        ).astype(jnp.bfloat16)


def products(gathered, left, right, groups):
    block = left.shape[0]
    vmem = pl.BlockSpec(memory_space=pltpu.VMEM)
    return pl.pallas_call(
        products_kernel,
        out_shape=jax.ShapeDtypeStruct((groups, block, block // groups), jnp.bfloat16),
        in_specs=[vmem] * 3,
        out_specs=vmem,
        compiler_params=pltpu.CompilerParams(vmem_limit_bytes=8 << 20),
        cost_estimate=pl.CostEstimate(
            flops=4 * block**3, bytes_accessed=8 * block**2, transcendentals=0
        ),
    )(gathered, left, right)


def returned_by_parts(gathered, left, bank, owners, my_columns):
    block = bank.shape[2]
    groups, workers = lax.axis_size("grp"), lax.axis_size("wk")
    me, worker = lax.axis_index("grp"), lax.axis_index("wk")
    size = workers // groups
    share = block // groups
    order = member_order(size)
    part = worker // size
    places = [looked_up(owner % size, np.argsort(order).tolist()) for owner in owners]

    column = 1 + jnp.sum(jnp.where(jnp.arange(groups) == me, my_columns, 0))
    right = in_order(pick(bank[0], column), order)
    left, right = lax.optimization_barrier((left, right))
    product = products(gathered, left, right, groups).reshape(workers, -1, share)

    parts = [
        [group * workers + index * size + int(place) for group in range(groups) for place in order]
        for index in range(groups)
    ]
    arrived = lax.all_to_all(
        product, ("grp", "wk"), 0, 0, axis_index_groups=parts, tiled=True
    ).reshape(groups, size, -1, share)

    def layers_of(index):
        return jnp.stack([pick(pick(arrived, index), place) for place in places])

    result = layers_of(part)
    for shift in range(1, groups):
        other = shifted(layers_of((part + shift) % groups), "wk", shift * size)
        source = (part + groups - shift) % groups
        theirs = jnp.stack([owner // size == source for owner in owners])
        result = jnp.where(theirs[:, None, None], other, result)
    return result


def returned_by_rows(gathered, left, bank, owners, my_columns):
    block = bank.shape[2]
    width = gathered.shape[1]
    groups, workers = lax.axis_size("grp"), lax.axis_size("wk")
    me = lax.axis_index("grp")
    share, blocks = block // groups, my_columns.shape[0]

    full = jnp.zeros((groups, share, width), jnp.bfloat16)
    for shift in reversed(range(groups)):
        rows = lax.dynamic_slice_in_dim(left, (me + shift) % groups * share, share, 1)
        product = transposed_dot(rows, gathered)
        product = shifted(product, "grp", shift) if shift else product
        source = (me + groups - shift) % groups
        full = lax.dynamic_update_slice_in_dim(full, product[None], source, 0)
    full = full.transpose(1, 0, 2).reshape(share, blocks, block)
    rights = jnp.stack([pick(bank[0], 1 + my_columns[index]) for index in range(blocks)])
    product = jnp.einsum("jab,rjb->jar", rights, full, preferred_element_type=jnp.float32)
    product = product.astype(jnp.bfloat16).reshape(workers, -1, share)
    arrived = lax.all_to_all(product, "wk", 0, 0, tiled=True)
    return jnp.stack([pick(arrived, owner) for owner in owners])


def on_device(grads, bank, owners, col_map):
    layers, _, total_width = grads.shape[1:]
    block = bank.shape[2]
    groups, workers = lax.axis_size("grp"), lax.axis_size("wk")
    me, worker = lax.axis_index("grp"), lax.axis_index("wk")
    width = total_width // groups
    order = member_order(workers)

    serves = owners[None, :] == order[:, None]

    def columns(group):
        return lax.dynamic_slice_in_dim(grads[0], group * width, width, 2)

    def placed(rows):
        placed_rows = jnp.broadcast_to(rows[0], (workers,) + rows.shape[1:])
        for layer in range(1, layers):
            placed_rows = jnp.where(serves[:, layer, None, None], rows[layer][None], placed_rows)
        return placed_rows.astype(jnp.float32)

    summed = placed(columns(me))
    for shift in range(1, groups):
        summed += placed(shifted(columns((me + shift) % groups), "grp", shift))
    outgoing = summed.astype(jnp.bfloat16)
    planes = [[group * workers + int(member) for member in order] for group in range(groups)]
    gathered = lax.all_to_all(
        outgoing, ("grp", "wk"), 0, 0, axis_index_groups=planes, tiled=True
    ).reshape(block, width)

    my_columns = jnp.sum(jnp.where((owners == worker)[:, None], col_map, 0), axis=0)
    owners = scalars_of(owners, workers)
    left = in_order(bank[0, 0], order)
    by_parts = width == block and workers % groups == 0
    returned = returned_by_parts if by_parts else returned_by_rows
    result = returned(gathered, left, bank, owners, my_columns)
    return result.astype(jnp.float32).transpose(0, 2, 1)


def solution(mesh):
    in_specs = (P("grp", None, "wk", None), P("wk", None, None, None), P(), P())
    out_specs = P(None, "grp", "wk")
    return jax.shard_map(
        on_device, mesh=mesh, in_specs=in_specs, out_specs=out_specs, check_vma=False
    )
```
